32 devices in a mesh: rows: 16 (over z, x, core), layer: 2 (over y).
Axes of the slice: x: 2, y: 2, z: 4, core: 2. Of those that a mesh axis runs over, the one named last changes fastest.
Arguments:
- gradients: float32 [4096, 32, 2880], P(('layer', 'rows')), parts along dimension 0, may hold values from -6 to 6
- in_basis: bfloat16 [5760, 2880], P(('layer', 'rows')), parts along dimension 0, may hold values from -0.109375 to 0.109375
- out_basis: bfloat16 [4096, 2048], P(('layer', 'rows')), parts along dimension 0, may hold values from -0.125 to 0.125
- eigen_seeds: int32 [5760, 2048], P(('layer', 'rows')), parts along dimension 0, may hold values from 0 to 63
Outputs:
- precond: float32 [4096, 92160], P('layer', 'rows'), parts along dimension 0
The draws below stay inside these ranges and needn't reach their ends.
There are 2 independent parts, one for each index of `layer`. The reference program is written for one: setup_inputs(seed, part) draws one part's arguments, and reference() takes and returns one part's arrays. A program takes and returns all parts, laid end to end along the dimension named above; each array names one. Nothing has to cross between parts.
All inputs are finite; a program needn't handle non-finite values.
Results may differ from the reference program's by a relative error of at most 0.0041.
Values may be sent and summed in bfloat16 or wider, within the bound.
No kernel may reach another device: no remote copies, remote signals or barrier semaphores. Data moves between devices by JAX's collectives and lax.ppermute only.
A program may use at most 256 MiB of HBM per device.

```python
import jax
import jax.numpy as jnp

DOUT = 2048
DIN = 2880
NG = 32


def touch_ends(entries, rng, least, top_value):
    longest = entries.shape.index(max(entries.shape))
    spots = []
    for shift in (0, 1):
        where = [jax.random.randint(jax.random.fold_in(rng, axis), (), 0, length) for axis, length in enumerate(entries.shape)]
        where[longest] = (where[longest] + shift) % entries.shape[longest]
        spots.append(tuple(where))
    return entries.at[spots[0]].set(least).at[spots[1]].set(top_value)


def steps_of(stream_key, extent, split, smallest, largest):
    def one(position, blocks):
        draws = jax.random.uniform(jax.random.fold_in(jax.random.fold_in(stream_key, 6), position), (blocks,), jnp.float32, smallest / len(split), largest / len(split))
        return jnp.repeat(jnp.exp(draws), extent[position] // blocks).reshape((-1,) + (1,) * (len(extent) - position - 1))

    factor_of = one(*split[0])
    for cut in split[1:]:
        factor_of = factor_of * one(*cut)
    return factor_of


def centred(key, dims, scale, most, shards=(), dtype=jnp.bfloat16):
    factor_of = steps_of(key, dims, shards, -0.22, 0.18) if shards else 1.0
    drawn = jax.random.normal(key, dims, jnp.float32) * scale * factor_of
    return jnp.minimum(jnp.maximum(drawn, -most), most).astype(dtype)


def setup_inputs(seed: int = 0, part: int = 0) -> dict:
    seeds = jax.random.split(jax.random.key(seed), 5)
    part_splits = jax.random.split(jax.random.fold_in(seeds[4], part), 5)
    return {
        "gradients": centred(part_splits[0], (DOUT, NG, DIN), 1.0, 6.0, ((0, 16),), jnp.float32),
        "in_basis": centred(part_splits[1], (DIN, DIN), DIN ** -0.5, 0.109375, ((0, 16),)),
        "out_basis": centred(part_splits[2], (DOUT, DOUT), DOUT ** -0.5, 0.125, ((0, 16),)),
        "eigen_seeds": touch_ends(jax.random.randint(part_splits[3], (DIN, DOUT), 0, 64), jax.random.fold_in(part_splits[3], 1), 0, 63).astype(jnp.int32),
    }


def reference(gradients, in_basis, out_basis, eigen_seeds):
    grad_low = gradients.astype(jnp.bfloat16).reshape(DOUT * NG, DIN)
    rotated = jnp.dot(grad_low, in_basis, preferred_element_type=jnp.float32).astype(jnp.bfloat16)
    rotated = rotated.reshape(DOUT, NG * DIN)
    both = jnp.dot(out_basis.T, rotated, preferred_element_type=jnp.float32)
    both = both.reshape(DOUT, NG, DIN).transpose(0, 2, 1)
    eigval = jnp.exp2(eigen_seeds.astype(jnp.float32) * 0.125 - 4.0)
    denom = (eigval + 0.1).T
    return (both / denom[:, :, None]).reshape(DOUT, DIN * NG)
```

```python
import functools

import jax
import jax.numpy as jnp
from jax import lax
from jax.experimental import pallas as pl
from jax.experimental.pallas import tpu as pltpu
from jax.sharding import PartitionSpec as P

LANES = 128
WEIGHTS = (2, 4, 6, 7, 7, 7, 6, 4, 2)
VMEM = 60 * 1024 * 1024


def chunk_units(units):
    total = sum(WEIGHTS)
    edges = [round(sum(WEIGHTS[:n]) * units / total) for n in range(len(WEIGHTS) + 1)]
    return [high - low for low, high in zip(edges, edges[1:]) if high > low]


def rotate_kernel(grads, first, *refs):
    if first:
        basis_ref, grad_ref, out_ref, low_ref, basis_t, rows = refs
    else:
        basis_ref, grad_ref, out_ref, basis_t, rows = refs
    step = pl.program_id(0)
    columns = basis_ref.shape[1]

    @pl.when(step == 0)
    def _():
        basis_t[...] = basis_ref[...].T

    if first:
        low_ref[0, :, :LANES] = grad_ref[0].astype(jnp.bfloat16)
        low_ref[0, :, LANES:] = grad_ref[1].astype(jnp.bfloat16)
        pair = low_ref[0]
    else:
        pair = grad_ref[0]
    product = jnp.dot(basis_t[...], pair, preferred_element_type=jnp.float32)
    for half in range(2):
        rows[pl.ds(2 * step + half, columns, stride=grads), :] = product[:, half * LANES : (half + 1) * LANES]

    @pl.when(step == pl.num_programs(0) - 1)
    def _():
        height = out_ref.shape[1]

        def flush(owner, carry):
            out_ref[owner] = rows[pl.ds(pl.multiple_of(owner * height, LANES), height), :].astype(jnp.bfloat16)
            return carry

        lax.fori_loop(0, out_ref.shape[0], flush, 0)


def rotate(basis, grad, devices, grads, first):
    depth, columns = basis.shape
    height = columns // devices * grads
    pairs = grads // 2
    out_shape = [jax.ShapeDtypeStruct((devices, height, LANES), jnp.bfloat16)]
    out_specs = [pl.BlockSpec((devices, height, LANES), lambda step: (0, 0, 0))]
    if first:
        grad_spec = pl.BlockSpec((2, depth, LANES), lambda step: (step, 0, 0))
        out_shape.append(jax.ShapeDtypeStruct((pairs, depth, 2 * LANES), jnp.bfloat16))
        out_specs.append(pl.BlockSpec((1, depth, 2 * LANES), lambda step: (step, 0, 0)))
    else:
        grad_spec = pl.BlockSpec((1, depth, 2 * LANES), lambda step: (step, 0, 0))
    return pl.pallas_call(
        functools.partial(rotate_kernel, grads, first),
        grid=(pairs,),
        in_specs=[pl.BlockSpec((depth, columns), lambda step: (0, 0)), grad_spec],
        out_specs=out_specs,
        out_shape=out_shape,
        scratch_shapes=[
            pltpu.VMEM((columns, depth), jnp.bfloat16),
            pltpu.VMEM((columns * grads, LANES), jnp.float32),
        ],
        compiler_params=pltpu.CompilerParams(vmem_limit_bytes=VMEM),
        cost_estimate=pl.CostEstimate(
            flops=2 * columns * depth * grads * LANES,
            bytes_accessed=2 * grads * depth * LANES * (3 if first else 1) + 2 * columns * (depth + grads * LANES),
            transcendentals=0,
        ),
    )(basis, grad)


def finish_kernel(begin, grads, *refs):
    basis_ref, moved_ref, scale_ref, out_ref = refs[0], refs[1], refs[2], refs[-1]
    devices = moved_ref.shape[0]
    moved = jnp.concatenate([moved_ref[source] for source in range(devices)], axis=1)
    both = lax.dot_general(basis_ref[...], moved, (((1,), (1,)), ((), ())), preferred_element_type=jnp.float32)
    per_block = LANES // grads
    height = both.shape[0]
    lane = lax.broadcasted_iota(jnp.int32, (height, LANES), 1) // grads
    for block in range(both.shape[1] // LANES):
        where = begin + block * per_block
        tile = scale_ref[:, where // LANES * LANES : (where // LANES + 1) * LANES]
        scale = jnp.take_along_axis(tile, lane + where % LANES, axis=1)
        part = slice(block * LANES, (block + 1) * LANES)
        out_ref[:, part] = both[:, part] * scale


def finish(basis_t, moved, scale, result, begin, span, grads):
    devices, height, _ = moved.shape
    width_out = basis_t.shape[0]
    tile = width_out // 4
    first_block = begin * grads // LANES
    aliased = [] if result is None else [result]
    return pl.pallas_call(
        functools.partial(finish_kernel, begin, grads),
        grid=(width_out // tile,),
        in_specs=[
            pl.BlockSpec((tile, basis_t.shape[1]), lambda row: (row, 0)),
            pl.BlockSpec(moved.shape, lambda row: (0, 0, 0)),
            pl.BlockSpec((tile, scale.shape[1]), lambda row: (row, 0)),
        ]
        + [pl.BlockSpec(memory_space=pl.ANY)] * len(aliased),
        out_specs=pl.BlockSpec((pl.Element(tile), pl.Element(height)), lambda row: (row * tile, first_block * LANES)),
        out_shape=jax.ShapeDtypeStruct((width_out, span * grads), jnp.float32),
        input_output_aliases={3: 0} if aliased else {},
        compiler_params=pltpu.CompilerParams(vmem_limit_bytes=VMEM),
        cost_estimate=pl.CostEstimate(
            flops=2 * width_out * height * basis_t.shape[1],
            bytes_accessed=2 * basis_t.size + 2 * moved.size + 4 * width_out * height,
            transcendentals=0,
        ),
    )(basis_t, moved, scale, *aliased)


def pipelined(gradients, in_basis, out_basis, eigen_seeds):
    devices = lax.axis_size("rows")
    local_rows, grads, width_in = gradients.shape
    span = width_in // devices
    step = LANES // grads
    counts = [step * n for n in chunk_units(span // step)]
    begins = [sum(counts[:n]) for n in range(len(counts))]

    def columns_of(begin, count):
        return [in_basis[:, owner * span + begin : owner * span + begin + count] for owner in range(devices)]

    def gathered(blocks):
        return lax.all_gather(blocks, "rows", axis=0, tiled=True)

    first_basis = gathered(jnp.concatenate(columns_of(0, counts[0]), axis=1))
    rest = [piece for begin, count in zip(begins[1:], counts[1:]) for piece in columns_of(begin, count)]
    rest_basis = gathered(jnp.concatenate(rest, axis=1))
    basis_t = gathered(out_basis).T
    denom = jnp.exp2(eigen_seeds.astype(jnp.float32) * 0.125 - 4.0) + 0.1
    scale = jnp.pad((1.0 / denom).T, ((0, 0), (0, -span % LANES)))

    grad = gradients.transpose(1, 2, 0)
    moved = []
    offset = 0
    low = None
    for n, count in enumerate(counts):
        if n == 0:
            rotated, low = rotate(first_basis, grad, devices, grads, True)
        else:
            basis = rest_basis[:, offset : offset + devices * count]
            offset += devices * count
            (rotated,) = rotate(basis, low, devices, grads, False)
        moved.append(lax.all_to_all(rotated, "rows", split_axis=0, concat_axis=0, tiled=True))
    result = None
    for n, begin in enumerate(begins):
        result = finish(basis_t, moved[n], scale, result, begin, span, grads)
    return result


def general(gradients, in_basis, out_basis, eigen_seeds):
    devices = lax.axis_size("rows")
    local_rows = gradients.shape[0]
    grads = gradients.shape[1]
    width_in = gradients.shape[2]
    span = width_in // devices
    grad_low = gradients.astype(jnp.bfloat16).reshape(local_rows * grads, width_in)
    full_in = lax.all_gather(in_basis, "rows", axis=0, tiled=True)
    rotated = jnp.dot(grad_low, full_in, preferred_element_type=jnp.float32)
    rotated = rotated.astype(jnp.bfloat16).reshape(local_rows, grads, devices, span)
    rotated = rotated.transpose(0, 2, 3, 1).reshape(local_rows, devices, span * grads)
    moved = lax.all_to_all(rotated, "rows", split_axis=1, concat_axis=0, tiled=True)
    width_out = moved.shape[0]
    moved = moved.reshape(width_out, span * grads)
    both = lax.dot_general(
        lax.all_gather(out_basis, "rows", axis=0, tiled=True),
        moved,
        (((0,), (0,)), ((), ())),
        preferred_element_type=jnp.float32,
    )
    eigval = jnp.exp2(eigen_seeds.astype(jnp.float32) * 0.125 - 4.0)
    denom = (eigval + 0.1).T
    result = both.reshape(width_out, span, grads) / denom[:, :, None]
    return result.reshape(width_out, span * grads)


def local(gradients, in_basis, out_basis, eigen_seeds):
    devices = lax.axis_size("rows")
    local_rows, grads, width_in = gradients.shape
    span = width_in // devices
    fits = local_rows == LANES and LANES % grads == 0 and grads % 16 == 0 and span * grads % LANES == 0
    return (pipelined if fits else general)(gradients, in_basis, out_basis, eigen_seeds)


def solution(mesh):
    placed = (
        P(("layer", "rows"), None, None),
        P(("layer", "rows"), None),
        P(("layer", "rows"), None),
        P(("layer", "rows"), None),
    )
    return jax.shard_map(
        local, mesh=mesh, in_specs=placed, out_specs=P("layer", "rows"), check_vma=False
    )
```

```python
import functools

import jax
import jax.numpy as jnp
from jax import lax
from jax.experimental import pallas as pl
from jax.experimental.pallas import tpu as pltpu
from jax.sharding import PartitionSpec as P


LANES = 128
WEIGHTS = (4, 8, 10, 10, 6, 4, 3)
GROUPS = (0, 1, 2)
VMEM = 60 * 1024 * 1024


def chunk_units(units):
    total = sum(WEIGHTS)
    edges = [round(sum(WEIGHTS[:n]) * units / total) for n in range(len(WEIGHTS) + 1)]
    return [high - low for low, high in zip(edges, edges[1:]) if high > low]


def full_tiles(columns):
    return -(-columns // LANES) * LANES


def exchange(block, flip):
    devices = lax.axis_size("rows")
    return lax.ppermute(block, "rows", [(source, source ^ flip) for source in range(devices)])


def far_bits(devices):
    return [1 << bit for bit in reversed(range(devices.bit_length() - 1))]


def offsets(devices):
    order = [0]
    for bit in far_bits(devices):
        order = order + [bit | other for other in order]
    return order


def gather_absolute(block):
    me = lax.axis_index("rows")
    for bit in far_bits(lax.axis_size("rows")):
        other = exchange(block, bit)
        low = (me & bit) == 0
        block = jnp.concatenate([jnp.where(low, block, other), jnp.where(low, other, block)])
    return block


def arrange_kernel(devices, spans, basis_ref, *outs):
    span = basis_ref.shape[1] // devices
    whole = basis_ref[...].astype(jnp.float32)
    for out_ref, group in zip(outs, spans):
        pieces = []
        for begin, count in group:
            pieces += [whole[:, owner * span + begin : owner * span + begin + count] for owner in range(devices)]
        blank = out_ref.shape[2] - sum(piece.shape[1] for piece in pieces)
        if blank:
            pieces.append(jnp.zeros((whole.shape[0], blank), jnp.float32))
        out_ref[0] = jnp.concatenate(pieces, axis=1).astype(jnp.bfloat16)


def arrange(in_basis, devices, spans):
    rows, _ = in_basis.shape
    return pl.pallas_call(
        functools.partial(arrange_kernel, devices, spans),
        out_shape=[
            jax.ShapeDtypeStruct((1, rows, full_tiles(devices * sum(count for _, count in group))), jnp.bfloat16)
            for group in spans
        ],
        compiler_params=pltpu.CompilerParams(vmem_limit_bytes=VMEM),
    )(in_basis)


def rotate_kernel(columns, grads, sources, order, me_ref, *refs):
    basis_ref, grad_ref = refs[:2]
    outs = refs[2 : 2 + len(order)]
    stage, basis_t, rows, pair = refs[-4:]
    step = pl.program_id(0)
    part = basis_ref.shape[1]

    @pl.when(step == 0)
    def _():
        for slot, source in enumerate(sources):
            stage[source * part : (source + 1) * part, :] = basis_ref[slot].astype(jnp.float32)
        basis_t[...] = stage[...].T.astype(jnp.bfloat16)

    pair[:, :LANES] = grad_ref[0].astype(jnp.bfloat16)
    pair[:, LANES:] = grad_ref[1].astype(jnp.bfloat16)
    product = jnp.dot(basis_t[:columns, :], pair[...], preferred_element_type=jnp.float32)
    for half in range(2):
        rows[pl.ds(2 * step + half, columns, stride=grads), :] = product[:, half * LANES : (half + 1) * LANES]

    @pl.when(step == pl.num_programs(0) - 1)
    def _():
        height = outs[0].shape[0]
        for out_ref, offset in zip(outs, order):
            owner = me_ref[0] ^ offset
            out_ref[...] = rows[pl.ds(pl.multiple_of(owner * height, LANES), height), :].astype(jnp.bfloat16)


def rotate(me, basis, begin, columns, grad, grads, sources, order):
    devices, part, _ = basis.shape
    depth = devices * part
    height = columns // devices * grads
    wide = full_tiles(columns)
    basis_spec = pl.BlockSpec(
        (pl.Element(devices), pl.Element(part), pl.Element(wide)), lambda step, me: (0, 0, begin)
    )
    return pl.pallas_call(
        functools.partial(rotate_kernel, columns, grads, sources, order),
        grid_spec=pltpu.PrefetchScalarGridSpec(
            num_scalar_prefetch=1,
            grid=(grads // 2,),
            in_specs=[basis_spec, pl.BlockSpec((2, depth, LANES), lambda step, me: (step, 0, 0))],
            out_specs=[pl.BlockSpec((height, LANES), lambda step, me: (0, 0))] * devices,
            scratch_shapes=[
                pltpu.VMEM((depth, wide), jnp.float32),
                pltpu.VMEM((wide, depth), jnp.bfloat16),
                pltpu.VMEM((columns * grads, LANES), jnp.float32),
                pltpu.VMEM((depth, 2 * LANES), jnp.bfloat16),
            ],
        ),
        out_shape=[jax.ShapeDtypeStruct((height, LANES), jnp.bfloat16)] * devices,
        compiler_params=pltpu.CompilerParams(vmem_limit_bytes=VMEM),
        cost_estimate=pl.CostEstimate(
            flops=2 * columns * depth * grads * LANES,
            bytes_accessed=4 * grads * depth * LANES + 2 * columns * (depth + grads * LANES),
            transcendentals=0,
        ),
    )(me, basis, grad)


def finish_kernel(begin, grads, devices, *refs):
    basis_ref, scale_ref, out_ref = refs[0], refs[1], refs[-1]
    moved = jnp.concatenate([ref[...] for ref in refs[2 : 2 + devices]], axis=1)
    basis = jnp.concatenate([basis_ref[slot] for slot in range(devices)], axis=1)
    both = lax.dot_general(basis, moved, (((1,), (1,)), ((), ())), preferred_element_type=jnp.float32)
    per_block = LANES // grads
    height = both.shape[0]
    lane = lax.broadcasted_iota(jnp.int32, (height, LANES), 1) // grads
    for block in range(both.shape[1] // LANES):
        where = begin + block * per_block
        tile = scale_ref[:, where // LANES * LANES : (where // LANES + 1) * LANES]
        scale = jnp.take_along_axis(tile, lane + where % LANES, axis=1)
        part = slice(block * LANES, (block + 1) * LANES)
        out_ref[:, part] = both[:, part] * scale


def finish(basis, scale, moved, result, begin, span, grads):
    devices, width_out, _ = basis.shape
    height, _ = moved[0].shape
    tile = width_out // 4
    aliased = [] if result is None else [result]
    return pl.pallas_call(
        functools.partial(finish_kernel, begin, grads, devices),
        grid=(width_out // tile,),
        in_specs=[
            pl.BlockSpec((devices, tile, LANES), lambda row: (0, row, 0)),
            pl.BlockSpec((tile, scale.shape[1]), lambda row: (row, 0)),
        ]
        + [pl.BlockSpec((height, LANES), lambda row: (0, 0))] * devices
        + [pl.BlockSpec(memory_space=pl.ANY)] * len(aliased),
        out_specs=pl.BlockSpec((pl.Element(tile), pl.Element(height)), lambda row: (row * tile, begin * grads)),
        out_shape=jax.ShapeDtypeStruct((width_out, span * grads), jnp.float32),
        input_output_aliases={2 + devices: 0} if aliased else {},
        compiler_params=pltpu.CompilerParams(vmem_limit_bytes=VMEM),
        cost_estimate=pl.CostEstimate(
            flops=2 * width_out * height * devices * LANES,
            bytes_accessed=2 * basis.size + 2 * devices * height * LANES + 4 * width_out * height,
            transcendentals=0,
        ),
    )(basis, scale, *moved, *aliased)


def pipelined(gradients, in_basis, out_basis, eigen_seeds):
    devices = lax.axis_size("rows")
    _, grads, width_in = gradients.shape
    span = width_in // devices
    step = LANES // grads
    counts = [step * n for n in chunk_units(span // step)]
    begins = [sum(counts[:n]) for n in range(len(counts))]
    chunks = list(zip(begins, counts))
    spans = [chunks[low:high] for low, high in zip(GROUPS, GROUPS[1:] + (len(chunks),))]
    order = offsets(devices)
    me = lax.axis_index("rows").astype(jnp.int32)[None]

    (early,) = arrange(in_basis, devices, spans[:1])
    gathered = [lax.all_gather(block, "rows", axis=0, tiled=True) for block in arrange(in_basis, devices, spans[1:])]
    early = gather_absolute(early)
    early, out_basis = lax.optimization_barrier((early, out_basis))
    gathered = [early] + gathered
    basis = out_basis.T[None]
    denom = jnp.exp2(eigen_seeds.astype(jnp.float32) * 0.125 - 4.0) + 0.1
    scale = jnp.pad((1.0 / denom).T, ((0, 0), (0, -span % LANES)))
    for n, bit in enumerate(far_bits(devices)):
        incoming = exchange(basis, bit)
        basis = jnp.concatenate([basis, incoming])

    grad = gradients.transpose(1, 2, 0)
    far = sorted(range(devices), key=lambda slot: -order[slot])
    moved = []
    for n, (begin, count) in enumerate(chunks):
        group = max(index for index, low in enumerate(GROUPS) if low <= n)
        column = (begin - begins[GROUPS[group]]) * devices
        sources = list(range(devices)) if group else order
        rotated = rotate(me, gathered[group], column, count * devices, grad, grads, sources, order)
        if n > 1:
            rotated, moved[n - 2], grad = lax.optimization_barrier((rotated, moved[n - 2], grad))
        arrived = {slot: exchange(rotated[slot], order[slot]) if order[slot] else rotated[slot] for slot in far}
        moved.append([arrived[slot] for slot in range(devices)])
    result = None
    for n, begin in enumerate(begins):
        result = finish(basis, scale, moved[n], result, begin, span, grads)
    return result


def general(gradients, in_basis, out_basis, eigen_seeds):
    devices = lax.axis_size("rows")
    local_rows = gradients.shape[0]
    grads = gradients.shape[1]
    width_in = gradients.shape[2]
    span = width_in // devices
    grad_low = gradients.astype(jnp.bfloat16).reshape(local_rows * grads, width_in)
    full_in = lax.all_gather(in_basis, "rows", axis=0, tiled=True)
    rotated = jnp.dot(grad_low, full_in, preferred_element_type=jnp.float32)
    rotated = rotated.astype(jnp.bfloat16).reshape(local_rows, grads, devices, span)
    rotated = rotated.transpose(0, 2, 3, 1).reshape(local_rows, devices, span * grads)
    moved = lax.all_to_all(rotated, "rows", split_axis=1, concat_axis=0, tiled=True)
    width_out = moved.shape[0]
    moved = moved.reshape(width_out, span * grads)
    both = lax.dot_general(
        lax.all_gather(out_basis, "rows", axis=0, tiled=True),
        moved,
        (((0,), (0,)), ((), ())),
        preferred_element_type=jnp.float32,
    )
    eigval = jnp.exp2(eigen_seeds.astype(jnp.float32) * 0.125 - 4.0)
    denom = (eigval + 0.1).T
    result = both.reshape(width_out, span, grads) / denom[:, :, None]
    return result.reshape(width_out, span * grads)


def local(gradients, in_basis, out_basis, eigen_seeds):
    devices = lax.axis_size("rows")
    local_rows, grads, width_in = gradients.shape
    span = width_in // devices
    fits = local_rows == LANES and LANES % grads == 0 and grads % 16 == 0 and span * grads % LANES == 0
    fits = fits and devices & (devices - 1) == 0
    return (pipelined if fits else general)(gradients, in_basis, out_basis, eigen_seeds)


def solution(mesh):
    placed = (
        P(("layer", "rows"), None, None),
        P(("layer", "rows"), None),
        P(("layer", "rows"), None),
        P(("layer", "rows"), None),
    )
    return jax.shard_map(
        local, mesh=mesh, in_specs=placed, out_specs=P("layer", "rows"), check_vma=False
    )
```

```python
import functools

import jax
import jax.numpy as jnp
from jax import lax
from jax.experimental import pallas as pl
from jax.experimental.pallas import tpu as pltpu
from jax.sharding import PartitionSpec as P


LANES = 128
SUBLANES = 16
WEIGHTS = (6, 8, 6, 10, 8, 4, 3)
GROUPS = (0, 1, 3)
VMEM = 60 * 1024 * 1024


def chunk_units(units):
    total = sum(WEIGHTS)
    edges = [round(sum(WEIGHTS[:n]) * units / total) for n in range(len(WEIGHTS) + 1)]
    return [high - low for low, high in zip(edges, edges[1:]) if high > low]


def full_tiles(columns):
    return -(-columns // LANES) * LANES


def full_rows(rows):
    return -(-rows // SUBLANES) * SUBLANES


def exchange(block, flip):
    devices = lax.axis_size("rows")
    return lax.ppermute(block, "rows", [(source, source ^ flip) for source in range(devices)])


def far_bits(devices):
    return [1 << bit for bit in reversed(range(devices.bit_length() - 1))]


def offsets(devices):
    order = [0]
    for bit in far_bits(devices):
        order = order + [bit | other for other in order]
    return order


def spread(block, gate=None):
    *bits, last = far_bits(lax.axis_size("rows"))
    for n, bit in enumerate(bits):
        other = exchange(block, bit)
        if gate is not None and n == 0:
            other, _ = lax.optimization_barrier((other, gate))
        block = jnp.concatenate([block, other])
    return block, exchange(block, last)


def turn_kernel(basis_ref, out_ref):
    out_ref[...] = basis_ref[...].T


def turn(basis):
    return pl.pallas_call(turn_kernel, out_shape=jax.ShapeDtypeStruct(basis.shape[::-1], basis.dtype))(basis)


def arrange_kernel(devices, spans, basis_ref, *outs):
    span = basis_ref.shape[1] // devices
    whole = basis_ref[...].astype(jnp.float32)
    for out_ref, group in zip(outs, spans):
        pieces = []
        for begin, count in group:
            pieces += [whole[:, owner * span + begin : owner * span + begin + count] for owner in range(devices)]
        blank = out_ref.shape[1] - sum(piece.shape[1] for piece in pieces)
        if blank:
            pieces.append(jnp.zeros((whole.shape[0], blank), jnp.float32))
        rows = whole.shape[0]
        out_ref[:rows, :] = jnp.concatenate(pieces, axis=1).astype(jnp.bfloat16)
        if rows < out_ref.shape[0]:
            out_ref[rows:, :] = jnp.zeros((out_ref.shape[0] - rows, out_ref.shape[1]), jnp.bfloat16)


def arrange(in_basis, devices, spans):
    rows, _ = in_basis.shape
    return pl.pallas_call(
        functools.partial(arrange_kernel, devices, spans),
        out_shape=[
            jax.ShapeDtypeStruct((full_rows(rows), full_tiles(devices * sum(count for _, count in group))), jnp.bfloat16)
            for group in spans
        ],
        compiler_params=pltpu.CompilerParams(vmem_limit_bytes=VMEM),
    )(in_basis)


def rotate_kernel(columns, part, grads, order, me_ref, *refs):
    own_ref, other_ref, grad_ref = refs[:3]
    outs = refs[3 : 3 + len(order)]
    stage, basis_t, rows, pair = refs[-4:]
    step = pl.program_id(0)
    pitch = full_rows(part)

    @pl.when(step == 0)
    def _():
        even = me_ref[0] % 2 == 0
        for slot, offset in enumerate(order[: len(order) // 2]):
            block = slice(slot * pitch, slot * pitch + part)
            own, other = own_ref[block, :].astype(jnp.float32), other_ref[block, :].astype(jnp.float32)
            both = jnp.concatenate([jnp.where(even, own, other), jnp.where(even, other, own)])
            start = pl.multiple_of((me_ref[0] ^ offset) // 2 * (2 * part), 8)
            stage[pl.ds(start, 2 * part), :] = both
        basis_t[...] = stage[...].T.astype(jnp.bfloat16)

    pair[:, :LANES] = grad_ref[0].astype(jnp.bfloat16)
    pair[:, LANES:] = grad_ref[1].astype(jnp.bfloat16)
    product = jnp.dot(basis_t[:columns, :], pair[...], preferred_element_type=jnp.float32)
    for half in range(2):
        rows[pl.ds(2 * step + half, columns, stride=grads), :] = product[:, half * LANES : (half + 1) * LANES]

    @pl.when(step == pl.num_programs(0) - 1)
    def _():
        height = outs[0].shape[0]
        for out_ref, offset in zip(outs, order):
            owner = me_ref[0] ^ offset
            out_ref[...] = rows[pl.ds(pl.multiple_of(owner * height, LANES), height), :].astype(jnp.bfloat16)


def rotate(me, basis, begin, columns, grad, grads, order):
    devices = len(order)
    depth = grad.shape[1]
    part = depth // devices
    height = columns // devices * grads
    wide = full_tiles(columns)
    basis_spec = pl.BlockSpec(
        (pl.Element(basis[0].shape[0]), pl.Element(wide)), lambda step, me: (0, begin)
    )
    return pl.pallas_call(
        functools.partial(rotate_kernel, columns, part, grads, order),
        grid_spec=pltpu.PrefetchScalarGridSpec(
            num_scalar_prefetch=1,
            grid=(grads // 2,),
            in_specs=[basis_spec, basis_spec, pl.BlockSpec((2, depth, LANES), lambda step, me: (step, 0, 0))],
            out_specs=[pl.BlockSpec((height, LANES), lambda step, me: (0, 0))] * devices,
            scratch_shapes=[
                pltpu.VMEM((depth, wide), jnp.float32),
                pltpu.VMEM((wide, depth), jnp.bfloat16),
                pltpu.VMEM((columns * grads, LANES), jnp.float32),
                pltpu.VMEM((depth, 2 * LANES), jnp.bfloat16),
            ],
        ),
        out_shape=[jax.ShapeDtypeStruct((height, LANES), jnp.bfloat16)] * devices,
        compiler_params=pltpu.CompilerParams(vmem_limit_bytes=VMEM),
        cost_estimate=pl.CostEstimate(
            flops=2 * columns * depth * grads * LANES,
            bytes_accessed=4 * grads * depth * LANES + 2 * columns * (depth + grads * LANES),
            transcendentals=0,
        ),
    )(me, *basis, grad)


def eigen_kernel(seeds_ref, out_ref):
    rows = seeds_ref.shape[0]
    eigval = jnp.exp2(seeds_ref[...].astype(jnp.float32) * 0.125 - 4.0)
    out_ref[:rows, :] = 1.0 / (eigval + 0.1)
    if rows < out_ref.shape[0]:
        out_ref[rows:, :] = jnp.zeros((out_ref.shape[0] - rows, out_ref.shape[1]), jnp.float32)


def eigen(eigen_seeds):
    return pl.pallas_call(
        eigen_kernel,
        out_shape=jax.ShapeDtypeStruct((full_tiles(eigen_seeds.shape[0]), eigen_seeds.shape[1]), jnp.float32),
    )(eigen_seeds)


def finish_kernel(begin, grads, devices, *refs):
    own_ref, other_ref, scale_ref, out_ref = refs[0], refs[1], refs[2], refs[-1]
    moved = jnp.concatenate([ref[...] for ref in refs[3 : 3 + devices]], axis=1)
    basis = jnp.concatenate([ref[slot] for ref in (own_ref, other_ref) for slot in range(devices // 2)], axis=1)
    both = lax.dot_general(basis, moved, (((1,), (1,)), ((), ())), preferred_element_type=jnp.float32)
    per_block = LANES // grads
    height = both.shape[0]
    lane = lax.broadcasted_iota(jnp.int32, (height, LANES), 1) // grads
    for block in range(both.shape[1] // LANES):
        where = begin + block * per_block
        tile = scale_ref[:, where // LANES * LANES : (where // LANES + 1) * LANES]
        scale = jnp.take_along_axis(tile, lane + where % LANES, axis=1)
        part = slice(block * LANES, (block + 1) * LANES)
        out_ref[:, part] = both[:, part] * scale


def finish(basis, scale, moved, result, begin, span, grads):
    half, width_out, _ = basis[0].shape
    devices = 2 * half
    height, _ = moved[0].shape
    tile = width_out // 4
    aliased = [] if result is None else [result]
    return pl.pallas_call(
        functools.partial(finish_kernel, begin, grads, devices),
        grid=(width_out // tile,),
        in_specs=[
            pl.BlockSpec((half, tile, LANES), lambda row: (0, row, 0)),
            pl.BlockSpec((half, tile, LANES), lambda row: (0, row, 0)),
            pl.BlockSpec((tile, scale.shape[1]), lambda row: (row, 0)),
        ]
        + [pl.BlockSpec((height, LANES), lambda row: (0, 0))] * devices
        + [pl.BlockSpec(memory_space=pl.ANY)] * len(aliased),
        out_specs=pl.BlockSpec((pl.Element(tile), pl.Element(height)), lambda row: (row * tile, begin * grads)),
        out_shape=jax.ShapeDtypeStruct((width_out, span * grads), jnp.float32),
        input_output_aliases={3 + devices: 0} if aliased else {},
        compiler_params=pltpu.CompilerParams(vmem_limit_bytes=VMEM),
        cost_estimate=pl.CostEstimate(
            flops=2 * width_out * height * devices * LANES,
            bytes_accessed=4 * basis[0].size + 2 * devices * height * LANES + 4 * width_out * height,
            transcendentals=0,
        ),
    )(*basis, scale, *moved, *aliased)


def pipelined(gradients, in_basis, out_basis, eigen_seeds):
    devices = lax.axis_size("rows")
    _, grads, width_in = gradients.shape
    span = width_in // devices
    step = LANES // grads
    counts = [step * n for n in chunk_units(span // step)]
    begins = [sum(counts[:n]) for n in range(len(counts))]
    chunks = list(zip(begins, counts))
    spans = [chunks[low:high] for low, high in zip(GROUPS, GROUPS[1:] + (len(chunks),))]
    order = offsets(devices)
    me = lax.axis_index("rows").astype(jnp.int32)[None]

    (early,) = arrange(in_basis, devices, spans[:1])
    middle, late = arrange(in_basis, devices, spans[1:])
    early = spread(early)
    gathered = [early, spread(middle, early[0]), spread(late)]
    basis = [block.reshape(devices // 2, -1, LANES) for block in spread(turn(out_basis))]
    scale = eigen(eigen_seeds)
    scale = turn(scale)
    grad = gradients.transpose(1, 2, 0)
    far = sorted(range(devices), key=lambda slot: -order[slot])
    moved = []
    for n, (begin, count) in enumerate(chunks):
        group = max(index for index, low in enumerate(GROUPS) if low <= n)
        column = (begin - begins[GROUPS[group]]) * devices
        rotated = rotate(me, gathered[group], column, count * devices, grad, grads, order)
        if n > 1:
            rotated, moved[n - 2], grad = lax.optimization_barrier((rotated, moved[n - 2], grad))
        arrived = {slot: exchange(rotated[slot], order[slot]) if order[slot] else rotated[slot] for slot in far}
        moved.append([arrived[slot] for slot in range(devices)])
    result = None
    for n, begin in enumerate(begins):
        result = finish(basis, scale, moved[n], result, begin, span, grads)
    return result


def general(gradients, in_basis, out_basis, eigen_seeds):
    devices = lax.axis_size("rows")
    local_rows = gradients.shape[0]
    grads = gradients.shape[1]
    width_in = gradients.shape[2]
    span = width_in // devices
    grad_low = gradients.astype(jnp.bfloat16).reshape(local_rows * grads, width_in)
    full_in = lax.all_gather(in_basis, "rows", axis=0, tiled=True)
    rotated = jnp.dot(grad_low, full_in, preferred_element_type=jnp.float32)
    rotated = rotated.astype(jnp.bfloat16).reshape(local_rows, grads, devices, span)
    rotated = rotated.transpose(0, 2, 3, 1).reshape(local_rows, devices, span * grads)
    moved = lax.all_to_all(rotated, "rows", split_axis=1, concat_axis=0, tiled=True)
    width_out = moved.shape[0]
    moved = moved.reshape(width_out, span * grads)
    both = lax.dot_general(
        lax.all_gather(out_basis, "rows", axis=0, tiled=True),
        moved,
        (((0,), (0,)), ((), ())),
        preferred_element_type=jnp.float32,
    )
    eigval = jnp.exp2(eigen_seeds.astype(jnp.float32) * 0.125 - 4.0)
    denom = (eigval + 0.1).T
    result = both.reshape(width_out, span, grads) / denom[:, :, None]
    return result.reshape(width_out, span * grads)


def local(gradients, in_basis, out_basis, eigen_seeds):
    devices = lax.axis_size("rows")
    local_rows, grads, width_in = gradients.shape
    span = width_in // devices
    fits = local_rows == LANES and LANES % grads == 0 and grads % 16 == 0 and span * grads % LANES == 0
    fits = fits and devices & (devices - 1) == 0
    return (pipelined if fits else general)(gradients, in_basis, out_basis, eigen_seeds)


def solution(mesh):
    placed = (
        P(("layer", "rows"), None, None),
        P(("layer", "rows"), None),
        P(("layer", "rows"), None),
        P(("layer", "rows"), None),
    )
    return jax.shard_map(
        local, mesh=mesh, in_specs=placed, out_specs=P("layer", "rows"), check_vma=False
    )
```

```python
import functools

import jax
import jax.numpy as jnp
from jax import lax
from jax.experimental import pallas as pl
from jax.experimental.pallas import tpu as pltpu
from jax.sharding import PartitionSpec as P


LANES = 128
SUBLANES = 16
WEIGHTS = (6, 8, 6, 10, 8, 4, 3)
GROUPS = (0, 1, 3)
VMEM = 60 * 1024 * 1024


def chunk_units(units):
    total = sum(WEIGHTS)
    edges = [round(sum(WEIGHTS[:n]) * units / total) for n in range(len(WEIGHTS) + 1)]
    return [high - low for low, high in zip(edges, edges[1:]) if high > low]


def full_tiles(columns):
    return -(-columns // LANES) * LANES


def full_rows(rows):
    return -(-rows // SUBLANES) * SUBLANES


def exchange(block, flip):
    devices = lax.axis_size("rows")
    return lax.ppermute(block, "rows", [(source, source ^ flip) for source in range(devices)])


def far_bits(devices):
    return [1 << bit for bit in reversed(range(devices.bit_length() - 1))]


def offsets(devices):
    order = [0]
    for bit in far_bits(devices):
        order = order + [bit | other for other in order]
    return order


def spread(block, gate=None):
    *bits, last = far_bits(lax.axis_size("rows"))
    for n, bit in enumerate(bits):
        other = exchange(block, bit)
        if gate is not None and n == 0:
            other, _ = lax.optimization_barrier((other, gate))
        block = jnp.concatenate([block, other])
    return block, exchange(block, last)


def turn_kernel(basis_ref, out_ref):
    out_ref[...] = basis_ref[...].T


def turn(basis):
    return pl.pallas_call(turn_kernel, out_shape=jax.ShapeDtypeStruct(basis.shape[::-1], basis.dtype))(basis)


def arrange_kernel(devices, spans, basis_ref, *outs):
    span = basis_ref.shape[1] // devices
    whole = basis_ref[...].astype(jnp.float32)
    for out_ref, group in zip(outs, spans):
        pieces = []
        for begin, count in group:
            pieces += [whole[:, owner * span + begin : owner * span + begin + count] for owner in range(devices)]
        blank = out_ref.shape[1] - sum(piece.shape[1] for piece in pieces)
        if blank:
            pieces.append(jnp.zeros((whole.shape[0], blank), jnp.float32))
        rows = whole.shape[0]
        out_ref[:rows, :] = jnp.concatenate(pieces, axis=1).astype(jnp.bfloat16)
        if rows < out_ref.shape[0]:
            out_ref[rows:, :] = jnp.zeros((out_ref.shape[0] - rows, out_ref.shape[1]), jnp.bfloat16)


def arrange(in_basis, devices, spans):
    rows, _ = in_basis.shape
    return pl.pallas_call(
        functools.partial(arrange_kernel, devices, spans),
        out_shape=[
            jax.ShapeDtypeStruct((full_rows(rows), full_tiles(devices * sum(count for _, count in group))), jnp.bfloat16)
            for group in spans
        ],
        compiler_params=pltpu.CompilerParams(vmem_limit_bytes=VMEM),
    )(in_basis)


def rotate_kernel(columns, part, grads, order, me_ref, *refs):
    own_ref, other_ref, grad_ref = refs[:3]
    outs = refs[3 : 3 + len(order)]
    stage, basis_t, rows, pair = refs[-4:]
    step = pl.program_id(0)
    pitch = full_rows(part)

    @pl.when(step == 0)
    def _():
        even = me_ref[0] % 2 == 0
        for slot, offset in enumerate(order[: len(order) // 2]):
            block = slice(slot * pitch, slot * pitch + part)
            own, other = own_ref[block, :].astype(jnp.float32), other_ref[block, :].astype(jnp.float32)
            both = jnp.concatenate([jnp.where(even, own, other), jnp.where(even, other, own)])
            start = pl.multiple_of((me_ref[0] ^ offset) // 2 * (2 * part), 8)
            stage[pl.ds(start, 2 * part), :] = both

        def turned(tile, carry):
            lanes = pl.ds(pl.multiple_of(tile * LANES, LANES), LANES)
            basis_t[lanes, :] = stage[:, lanes].T.astype(jnp.bfloat16)
            return carry

        lax.fori_loop(0, stage.shape[1] // LANES, turned, 0)

    pair[:, :LANES] = grad_ref[0].astype(jnp.bfloat16)
    pair[:, LANES:] = grad_ref[1].astype(jnp.bfloat16)
    product = jnp.dot(basis_t[:columns, :], pair[...], preferred_element_type=jnp.float32)
    for half in range(2):
        rows[pl.ds(2 * step + half, columns, stride=grads), :] = product[:, half * LANES : (half + 1) * LANES]

    @pl.when(step == pl.num_programs(0) - 1)
    def _():
        height = outs[0].shape[0]
        for out_ref, offset in zip(outs, order):
            owner = me_ref[0] ^ offset
            out_ref[...] = rows[pl.ds(pl.multiple_of(owner * height, LANES), height), :].astype(jnp.bfloat16)


def rotate(me, basis, begin, columns, grad, grads, order):
    devices = len(order)
    depth = grad.shape[1]
    part = depth // devices
    height = columns // devices * grads
    wide = full_tiles(columns)
    basis_spec = pl.BlockSpec(
        (pl.Element(basis[0].shape[0]), pl.Element(wide)), lambda step, me: (0, begin)
    )
    return pl.pallas_call(
        functools.partial(rotate_kernel, columns, part, grads, order),
        grid_spec=pltpu.PrefetchScalarGridSpec(
            num_scalar_prefetch=1,
            grid=(grads // 2,),
            in_specs=[basis_spec, basis_spec, pl.BlockSpec((2, depth, LANES), lambda step, me: (step, 0, 0))],
            out_specs=[pl.BlockSpec((height, LANES), lambda step, me: (0, 0))] * devices,
            scratch_shapes=[
                pltpu.VMEM((depth, wide), jnp.float32),
                pltpu.VMEM((wide, depth), jnp.bfloat16),
                pltpu.VMEM((columns * grads, LANES), jnp.float32),
                pltpu.VMEM((depth, 2 * LANES), jnp.bfloat16),
            ],
        ),
        out_shape=[jax.ShapeDtypeStruct((height, LANES), jnp.bfloat16)] * devices,
        compiler_params=pltpu.CompilerParams(vmem_limit_bytes=VMEM),
        cost_estimate=pl.CostEstimate(
            flops=2 * columns * depth * grads * LANES,
            bytes_accessed=4 * grads * depth * LANES + 2 * columns * (depth + grads * LANES),
            transcendentals=0,
        ),
    )(me, *basis, grad)


def eigen_kernel(seeds_ref, out_ref):
    rows = seeds_ref.shape[0]
    eigval = jnp.exp2(seeds_ref[...].astype(jnp.float32) * 0.125 - 4.0)
    out_ref[:rows, :] = 1.0 / (eigval + 0.1)
    if rows < out_ref.shape[0]:
        out_ref[rows:, :] = jnp.zeros((out_ref.shape[0] - rows, out_ref.shape[1]), jnp.float32)


def eigen(eigen_seeds):
    return pl.pallas_call(
        eigen_kernel,
        out_shape=jax.ShapeDtypeStruct((full_tiles(eigen_seeds.shape[0]), eigen_seeds.shape[1]), jnp.float32),
    )(eigen_seeds)


def finish_kernel(begin, grads, devices, *refs):
    own_ref, other_ref, scale_ref, out_ref = refs[0], refs[1], refs[2], refs[-1]
    moved = jnp.concatenate([ref[...] for ref in refs[3 : 3 + devices]], axis=1)
    basis = jnp.concatenate([ref[slot] for ref in (own_ref, other_ref) for slot in range(devices // 2)], axis=1)
    both = lax.dot_general(basis, moved, (((1,), (1,)), ((), ())), preferred_element_type=jnp.float32)
    per_block = LANES // grads
    height = both.shape[0]
    lane = lax.broadcasted_iota(jnp.int32, (height, LANES), 1) // grads
    for block in range(both.shape[1] // LANES):
        where = begin + block * per_block
        tile = scale_ref[:, where // LANES * LANES : (where // LANES + 1) * LANES]
        scale = jnp.take_along_axis(tile, lane + where % LANES, axis=1)
        part = slice(block * LANES, (block + 1) * LANES)
        out_ref[:, part] = both[:, part] * scale


def finish(basis, scale, moved, result, begin, span, grads):
    half, width_out, _ = basis[0].shape
    devices = 2 * half
    height, _ = moved[0].shape
    tile = width_out // 4
    aliased = [] if result is None else [result]
    return pl.pallas_call(
        functools.partial(finish_kernel, begin, grads, devices),
        grid=(width_out // tile,),
        in_specs=[
            pl.BlockSpec((half, tile, LANES), lambda row: (0, row, 0)),
            pl.BlockSpec((half, tile, LANES), lambda row: (0, row, 0)),
            pl.BlockSpec((tile, scale.shape[1]), lambda row: (row, 0)),
        ]
        + [pl.BlockSpec((height, LANES), lambda row: (0, 0))] * devices
        + [pl.BlockSpec(memory_space=pl.ANY)] * len(aliased),
        out_specs=pl.BlockSpec((pl.Element(tile), pl.Element(height)), lambda row: (row * tile, begin * grads)),
        out_shape=jax.ShapeDtypeStruct((width_out, span * grads), jnp.float32),
        input_output_aliases={3 + devices: 0} if aliased else {},
        compiler_params=pltpu.CompilerParams(vmem_limit_bytes=VMEM),
        cost_estimate=pl.CostEstimate(
            flops=2 * width_out * height * devices * LANES,
            bytes_accessed=4 * basis[0].size + 2 * devices * height * LANES + 4 * width_out * height,
            transcendentals=0,
        ),
    )(*basis, scale, *moved, *aliased)


def pipelined(gradients, in_basis, out_basis, eigen_seeds):
    devices = lax.axis_size("rows")
    _, grads, width_in = gradients.shape
    span = width_in // devices
    step = LANES // grads
    counts = [step * n for n in chunk_units(span // step)]
    begins = [sum(counts[:n]) for n in range(len(counts))]
    chunks = list(zip(begins, counts))
    spans = [chunks[low:high] for low, high in zip(GROUPS, GROUPS[1:] + (len(chunks),))]
    order = offsets(devices)
    me = lax.axis_index("rows").astype(jnp.int32)[None]

    (early,) = arrange(in_basis, devices, spans[:1])
    middle, late = arrange(in_basis, devices, spans[1:])
    early = spread(early)
    gathered = [early, spread(middle, early[0]), spread(late)]
    out_basis = turn(out_basis)
    basis = [block.reshape(devices // 2, -1, LANES) for block in spread(out_basis)]
    scale = eigen(eigen_seeds)
    scale = turn(scale)
    grad = gradients.transpose(1, 2, 0)
    far = sorted(range(devices), key=lambda slot: -order[slot])
    moved = []
    for n, (begin, count) in enumerate(chunks):
        group = max(index for index, low in enumerate(GROUPS) if low <= n)
        column = (begin - begins[GROUPS[group]]) * devices
        rotated = rotate(me, gathered[group], column, count * devices, grad, grads, order)
        if n > 1:
            rotated, moved[n - 2], grad = lax.optimization_barrier((rotated, moved[n - 2], grad))
        arrived = {slot: exchange(rotated[slot], order[slot]) if order[slot] else rotated[slot] for slot in far}
        moved.append([arrived[slot] for slot in range(devices)])
    result = None
    for n, begin in enumerate(begins):
        result = finish(basis, scale, moved[n], result, begin, span, grads)
    return result


def general(gradients, in_basis, out_basis, eigen_seeds):
    devices = lax.axis_size("rows")
    local_rows = gradients.shape[0]
    grads = gradients.shape[1]
    width_in = gradients.shape[2]
    span = width_in // devices
    grad_low = gradients.astype(jnp.bfloat16).reshape(local_rows * grads, width_in)
    full_in = lax.all_gather(in_basis, "rows", axis=0, tiled=True)
    rotated = jnp.dot(grad_low, full_in, preferred_element_type=jnp.float32)
    rotated = rotated.astype(jnp.bfloat16).reshape(local_rows, grads, devices, span)
    rotated = rotated.transpose(0, 2, 3, 1).reshape(local_rows, devices, span * grads)
    moved = lax.all_to_all(rotated, "rows", split_axis=1, concat_axis=0, tiled=True)
    width_out = moved.shape[0]
    moved = moved.reshape(width_out, span * grads)
    both = lax.dot_general(
        lax.all_gather(out_basis, "rows", axis=0, tiled=True),
        moved,
        (((0,), (0,)), ((), ())),
        preferred_element_type=jnp.float32,
    )
    eigval = jnp.exp2(eigen_seeds.astype(jnp.float32) * 0.125 - 4.0)
    denom = (eigval + 0.1).T
    result = both.reshape(width_out, span, grads) / denom[:, :, None]
    return result.reshape(width_out, span * grads)


def local(gradients, in_basis, out_basis, eigen_seeds):
    devices = lax.axis_size("rows")
    local_rows, grads, width_in = gradients.shape
    span = width_in // devices
    fits = local_rows == LANES and LANES % grads == 0 and grads % 16 == 0 and span * grads % LANES == 0
    fits = fits and devices & (devices - 1) == 0
    return (pipelined if fits else general)(gradients, in_basis, out_basis, eigen_seeds)


def solution(mesh):
    placed = (
        P(("layer", "rows"), None, None),
        P(("layer", "rows"), None),
        P(("layer", "rows"), None),
        P(("layer", "rows"), None),
    )
    return jax.shard_map(
        local, mesh=mesh, in_specs=placed, out_specs=P("layer", "rows"), check_vma=False
    )
```

```python
import functools

import jax
import jax.numpy as jnp
from jax import lax
from jax.experimental import pallas as pl
from jax.experimental.pallas import tpu as pltpu
from jax.sharding import PartitionSpec as P


LANES = 128
SUBLANES = 16
WEIGHTS = (6, 8, 6, 10, 8, 4, 3)
GROUPS = (0, 1, 3)
SLICE = 1536
PER_STEP = 4
VMEM = 60 * 1024 * 1024


def chunk_units(units):
    total = sum(WEIGHTS)
    edges = [round(sum(WEIGHTS[:n]) * units / total) for n in range(len(WEIGHTS) + 1)]
    return [high - low for low, high in zip(edges, edges[1:]) if high > low]


def full_tiles(columns):
    return -(-columns // LANES) * LANES


def full_rows(rows):
    return -(-rows // SUBLANES) * SUBLANES


def exchange(block, flip):
    devices = lax.axis_size("rows")
    return lax.ppermute(block, "rows", [(source, source ^ flip) for source in range(devices)])


def far_bits(devices):
    return [1 << bit for bit in reversed(range(devices.bit_length() - 1))]


def offsets(devices):
    order = [0]
    for bit in far_bits(devices):
        order = order + [bit | other for other in order]
    return order


def spread(block, gate=None):
    *bits, last = far_bits(lax.axis_size("rows"))
    for n, bit in enumerate(bits):
        other = exchange(block, bit)
        if gate is not None and n == 0:
            other, _ = lax.optimization_barrier((other, gate))
        block = jnp.concatenate([block, other])
    return block, exchange(block, last)


def turn_kernel(basis_ref, out_ref):
    out_ref[...] = basis_ref[...].T


def turn(basis):
    return pl.pallas_call(turn_kernel, out_shape=jax.ShapeDtypeStruct(basis.shape[::-1], basis.dtype))(basis)


def arrange_kernel(devices, spans, basis_ref, *outs):
    span = basis_ref.shape[1] // devices
    whole = basis_ref[...].astype(jnp.float32)
    for out_ref, group in zip(outs, spans):
        pieces = []
        for begin, count in group:
            pieces += [whole[:, owner * span + begin : owner * span + begin + count] for owner in range(devices)]
        blank = out_ref.shape[1] - sum(piece.shape[1] for piece in pieces)
        if blank:
            pieces.append(jnp.zeros((whole.shape[0], blank), jnp.float32))
        rows = whole.shape[0]
        out_ref[:rows, :] = jnp.concatenate(pieces, axis=1).astype(jnp.bfloat16)
        if rows < out_ref.shape[0]:
            out_ref[rows:, :] = jnp.zeros((out_ref.shape[0] - rows, out_ref.shape[1]), jnp.bfloat16)


def arrange(in_basis, devices, spans):
    rows, _ = in_basis.shape
    return pl.pallas_call(
        functools.partial(arrange_kernel, devices, spans),
        out_shape=[
            jax.ShapeDtypeStruct((full_rows(rows), full_tiles(devices * sum(count for _, count in group))), jnp.bfloat16)
            for group in spans
        ],
        compiler_params=pltpu.CompilerParams(vmem_limit_bytes=VMEM),
    )(in_basis)


def rotate_kernel(columns, part, grads, order, me_ref, *refs):
    own_ref, other_ref, grad_ref = refs[:3]
    outs = refs[3 : 3 + len(order)]
    stage, basis_t, rows = refs[-3:]
    step = pl.program_id(0)
    pitch = full_rows(part)

    @pl.when(step == 0)
    def _():
        even = me_ref[0] % 2 == 0
        for slot, offset in enumerate(order[: len(order) // 2]):
            block = slice(slot * pitch, slot * pitch + part)
            own, other = own_ref[block, :].astype(jnp.float32), other_ref[block, :].astype(jnp.float32)
            both = jnp.concatenate([jnp.where(even, own, other), jnp.where(even, other, own)])
            start = pl.multiple_of((me_ref[0] ^ offset) // 2 * (2 * part), 8)
            stage[pl.ds(start, 2 * part), :] = both

        def turned(tile, carry):
            lanes = pl.ds(pl.multiple_of(tile * LANES, LANES), LANES)
            basis_t[lanes, :] = stage[:, lanes].T.astype(jnp.bfloat16)
            return carry

        lax.fori_loop(0, stage.shape[1] // LANES, turned, 0)

    for first in range(0, PER_STEP, 2):
        product = None
        for low in range(0, grad_ref.shape[1], SLICE):
            depth = slice(low, min(low + SLICE, grad_ref.shape[1]))
            pair = jnp.concatenate([grad_ref[first + half, depth, :].astype(jnp.bfloat16) for half in range(2)], axis=1)
            term = jnp.dot(basis_t[:columns, depth], pair, preferred_element_type=jnp.float32)
            product = term if product is None else product + term
        for half in range(2):
            place = pl.ds(PER_STEP * step + first + half, columns, stride=grads)
            rows[place, :] = product[:, half * LANES : (half + 1) * LANES]

    @pl.when(step == pl.num_programs(0) - 1)
    def _():
        height = outs[0].shape[0]
        for out_ref, offset in zip(outs, order):
            owner = me_ref[0] ^ offset
            out_ref[...] = rows[pl.ds(pl.multiple_of(owner * height, LANES), height), :].astype(jnp.bfloat16)


def rotate(me, basis, begin, columns, grad, grads, order):
    devices = len(order)
    depth = grad.shape[1]
    part = depth // devices
    height = columns // devices * grads
    wide = full_tiles(columns)
    basis_spec = pl.BlockSpec(
        (pl.Element(basis[0].shape[0]), pl.Element(wide)), lambda step, me: (0, begin)
    )
    return pl.pallas_call(
        functools.partial(rotate_kernel, columns, part, grads, order),
        grid_spec=pltpu.PrefetchScalarGridSpec(
            num_scalar_prefetch=1,
            grid=(grads // PER_STEP,),
            in_specs=[basis_spec, basis_spec, pl.BlockSpec((PER_STEP, depth, LANES), lambda step, me: (step, 0, 0))],
            out_specs=[pl.BlockSpec((height, LANES), lambda step, me: (0, 0))] * devices,
            scratch_shapes=[
                pltpu.VMEM((depth, wide), jnp.float32),
                pltpu.VMEM((wide, depth), jnp.bfloat16),
                pltpu.VMEM((columns * grads, LANES), jnp.float32),
            ],
        ),
        out_shape=[jax.ShapeDtypeStruct((height, LANES), jnp.bfloat16)] * devices,
        compiler_params=pltpu.CompilerParams(vmem_limit_bytes=VMEM),
        cost_estimate=pl.CostEstimate(
            flops=2 * columns * depth * grads * LANES,
            bytes_accessed=4 * grads * depth * LANES + 2 * columns * (depth + grads * LANES),
            transcendentals=0,
        ),
    )(me, *basis, grad)


def eigen_kernel(seeds_ref, out_ref):
    rows = seeds_ref.shape[0]
    eigval = jnp.exp2(seeds_ref[...].astype(jnp.float32) * 0.125 - 4.0)
    out_ref[:rows, :] = 1.0 / (eigval + 0.1)
    if rows < out_ref.shape[0]:
        out_ref[rows:, :] = jnp.zeros((out_ref.shape[0] - rows, out_ref.shape[1]), jnp.float32)


def eigen(eigen_seeds):
    return pl.pallas_call(
        eigen_kernel,
        out_shape=jax.ShapeDtypeStruct((full_tiles(eigen_seeds.shape[0]), eigen_seeds.shape[1]), jnp.float32),
    )(eigen_seeds)


def finish_kernel(begin, grads, devices, *refs):
    own_ref, other_ref, scale_ref, out_ref = refs[0], refs[1], refs[2], refs[-1]
    moved = jnp.concatenate([ref[...] for ref in refs[3 : 3 + devices]], axis=1)
    basis = jnp.concatenate([ref[slot] for ref in (own_ref, other_ref) for slot in range(devices // 2)], axis=1)
    both = lax.dot_general(basis, moved, (((1,), (1,)), ((), ())), preferred_element_type=jnp.float32)
    per_block = LANES // grads
    height = both.shape[0]
    lane = lax.broadcasted_iota(jnp.int32, (height, LANES), 1) // grads
    for block in range(both.shape[1] // LANES):
        where = begin + block * per_block
        tile = scale_ref[:, where // LANES * LANES : (where // LANES + 1) * LANES]
        scale = jnp.take_along_axis(tile, lane + where % LANES, axis=1)
        part = slice(block * LANES, (block + 1) * LANES)
        out_ref[:, part] = both[:, part] * scale


def finish(basis, scale, moved, result, begin, span, grads):
    half, width_out, _ = basis[0].shape
    devices = 2 * half
    height, _ = moved[0].shape
    tile = width_out // 4
    aliased = [] if result is None else [result]
    return pl.pallas_call(
        functools.partial(finish_kernel, begin, grads, devices),
        grid=(width_out // tile,),
        in_specs=[
            pl.BlockSpec((half, tile, LANES), lambda row: (0, row, 0)),
            pl.BlockSpec((half, tile, LANES), lambda row: (0, row, 0)),
            pl.BlockSpec((tile, scale.shape[1]), lambda row: (row, 0)),
        ]
        + [pl.BlockSpec((height, LANES), lambda row: (0, 0))] * devices
        + [pl.BlockSpec(memory_space=pl.ANY)] * len(aliased),
        out_specs=pl.BlockSpec((pl.Element(tile), pl.Element(height)), lambda row: (row * tile, begin * grads)),
        out_shape=jax.ShapeDtypeStruct((width_out, span * grads), jnp.float32),
        input_output_aliases={3 + devices: 0} if aliased else {},
        compiler_params=pltpu.CompilerParams(vmem_limit_bytes=VMEM),
        cost_estimate=pl.CostEstimate(
            flops=2 * width_out * height * devices * LANES,
            bytes_accessed=4 * basis[0].size + 2 * devices * height * LANES + 4 * width_out * height,
            transcendentals=0,
        ),
    )(*basis, scale, *moved, *aliased)


def pipelined(gradients, in_basis, out_basis, eigen_seeds):
    devices = lax.axis_size("rows")
    _, grads, width_in = gradients.shape
    span = width_in // devices
    step = LANES // grads
    counts = [step * n for n in chunk_units(span // step)]
    begins = [sum(counts[:n]) for n in range(len(counts))]
    chunks = list(zip(begins, counts))
    spans = [chunks[low:high] for low, high in zip(GROUPS, GROUPS[1:] + (len(chunks),))]
    order = offsets(devices)
    me = lax.axis_index("rows").astype(jnp.int32)[None]

    (early,) = arrange(in_basis, devices, spans[:1])
    middle, late = arrange(in_basis, devices, spans[1:])
    early = spread(early)
    gathered = [early, spread(middle, early[0]), spread(late)]
    out_basis = turn(out_basis)
    basis = [block.reshape(devices // 2, -1, LANES) for block in spread(out_basis)]
    scale = eigen(eigen_seeds)
    scale = turn(scale)
    grad = gradients.transpose(1, 2, 0)
    far = sorted(range(devices), key=lambda slot: -order[slot])
    moved = []
    for n, (begin, count) in enumerate(chunks):
        group = max(index for index, low in enumerate(GROUPS) if low <= n)
        column = (begin - begins[GROUPS[group]]) * devices
        rotated = rotate(me, gathered[group], column, count * devices, grad, grads, order)
        if n > 1:
            rotated, moved[n - 2], grad = lax.optimization_barrier((rotated, moved[n - 2], grad))
        arrived = {slot: exchange(rotated[slot], order[slot]) if order[slot] else rotated[slot] for slot in far}
        moved.append([arrived[slot] for slot in range(devices)])
    result = None
    for n, begin in enumerate(begins):
        result = finish(basis, scale, moved[n], result, begin, span, grads)
    return result


def general(gradients, in_basis, out_basis, eigen_seeds):
    devices = lax.axis_size("rows")
    local_rows = gradients.shape[0]
    grads = gradients.shape[1]
    width_in = gradients.shape[2]
    span = width_in // devices
    grad_low = gradients.astype(jnp.bfloat16).reshape(local_rows * grads, width_in)
    full_in = lax.all_gather(in_basis, "rows", axis=0, tiled=True)
    rotated = jnp.dot(grad_low, full_in, preferred_element_type=jnp.float32)
    rotated = rotated.astype(jnp.bfloat16).reshape(local_rows, grads, devices, span)
    rotated = rotated.transpose(0, 2, 3, 1).reshape(local_rows, devices, span * grads)
    moved = lax.all_to_all(rotated, "rows", split_axis=1, concat_axis=0, tiled=True)
    width_out = moved.shape[0]
    moved = moved.reshape(width_out, span * grads)
    both = lax.dot_general(
        lax.all_gather(out_basis, "rows", axis=0, tiled=True),
        moved,
        (((0,), (0,)), ((), ())),
        preferred_element_type=jnp.float32,
    )
    eigval = jnp.exp2(eigen_seeds.astype(jnp.float32) * 0.125 - 4.0)
    denom = (eigval + 0.1).T
    result = both.reshape(width_out, span, grads) / denom[:, :, None]
    return result.reshape(width_out, span * grads)


def local(gradients, in_basis, out_basis, eigen_seeds):
    devices = lax.axis_size("rows")
    local_rows, grads, width_in = gradients.shape
    span = width_in // devices
    fits = local_rows == LANES and LANES % grads == 0 and grads % 16 == 0 and span * grads % LANES == 0
    fits = fits and devices & (devices - 1) == 0
    return (pipelined if fits else general)(gradients, in_basis, out_basis, eigen_seeds)


def solution(mesh):
    placed = (
        P(("layer", "rows"), None, None),
        P(("layer", "rows"), None),
        P(("layer", "rows"), None),
        P(("layer", "rows"), None),
    )
    return jax.shard_map(
        local, mesh=mesh, in_specs=placed, out_specs=P("layer", "rows"), check_vma=False
    )
```
